32 devices in a mesh: rows: 16 (over z, y, x), rep: 2 (over core).
Axes of the slice: x: 2, y: 2, z: 4, core: 2. Of those that a mesh axis runs over, the one named last changes fastest.
Arguments:
- features: bfloat16 [4096, 128], P(('rows', 'rep')), may hold values from -6 to 6
- tile_counts: int32 [4096, 128, 128], P(('rows', 'rep')), may hold values from 0 to 3, as said below
- tile_row: int32 [4096], P(('rows', 'rep')), may hold values from 0 to 1
- tile_col: int32 [4096], P(('rows', 'rep')), may hold values from 0 to 31, as said below
- label_ids: int32 [2048], P(('rows', 'rep')), may hold values from 0 to 4095, as said below
- cotangent: bfloat16 [4096, 256], P(('rows', 'rep')), may hold values from -6 to 6
- self_weight: bfloat16 [128, 256], replicated, may hold values from -0.5 to 0.5
- neigh_weight: bfloat16 [128, 256], replicated, may hold values from -0.5 to 0.5
Outputs:
- activation: bfloat16 [4096, 256], P(('rows', 'rep'))
- grad_features: float32 [4096, 128], P(('rows', 'rep'))
- grad_self: float32 [128, 256], replicated
- grad_neigh: float32 [128, 256], replicated
The draws below stay inside these ranges and needn't reach their ends.
Inputs may be any that keep to these rules, and one draw needn't show every extreme that they name: `tile_counts`: edge counts of one tile; most entries are zero. `tile_col`: every tile held by a device of rep index c names a column block of the feature rows of some device of rep index c. On each device, at most 16 tiles name column blocks held by devices of one rows index, and exactly 16 do for some rows index. `label_ids`: the ids of one device's 64 labels are distinct and lie among that device's own feature rows.
All inputs are finite; a program needn't handle non-finite values.
Results may differ from the reference program's by a relative error of at most 0.0053.
Values may be sent and summed in bfloat16 or wider, within the bound.
A program may use at most 128 MiB of HBM per device.

```python
import jax
import jax.numpy as jnp
from jax import lax

F_IN = 128
HID = 256
BLOCK = 128
NODES_DEV = 256
TILE_DEV = 128
HALF = 128
CAP = 16
LAB_DEV = 64
NODES = 4096
TILES = 4096
LABELS = 2048
N_ROWS = 16
N_REP = 2


def draw_tile_counts(key, part):
    present = jax.random.randint(key, (TILES, BLOCK, BLOCK), 0, 32, dtype=jnp.int32) == 0
    values = jax.random.randint(jax.random.fold_in(key, 1), (TILES, BLOCK, BLOCK), 1, 4, dtype=jnp.int32)
    return jnp.where(present, values, 0).astype(jnp.int32)


def draw_tile_col(key, part):
    per_half = HALF // BLOCK
    slot_total = CAP * N_ROWS

    def single(which):
        device_key = jax.random.fold_in(key, which)
        replica = which % N_REP
        owner_order = jax.random.permutation(jax.random.fold_in(device_key, 1), N_ROWS).astype(jnp.int32)
        slot_owner = owner_order[jnp.arange(slot_total, dtype=jnp.int32) // CAP]
        rest = jax.random.permutation(jax.random.fold_in(device_key, 2), slot_total - CAP).astype(jnp.int32)[:TILE_DEV - CAP] + CAP
        chosen = jnp.concatenate([jnp.arange(CAP, dtype=jnp.int32), rest])
        owners = slot_owner[chosen]
        shuffle = jax.random.permutation(jax.random.fold_in(device_key, 3), TILE_DEV).astype(jnp.int32)
        owners = owners[shuffle]
        within = jax.random.randint(jax.random.fold_in(device_key, 4), (TILE_DEV,), 0, per_half, dtype=jnp.int32)
        return ((owners * N_REP + replica) * per_half + within).astype(jnp.int32)
    return jax.vmap(single)(jnp.arange(N_ROWS * N_REP, dtype=jnp.int32)).reshape(-1).astype(jnp.int32)


def draw_label_ids(key, part):

    def single(which):
        shuffled = jax.random.permutation(jax.random.fold_in(key, which), HALF)
        return shuffled[:LAB_DEV].astype(jnp.int32) + which * HALF
    return jax.vmap(single)(jnp.arange(N_ROWS * N_REP, dtype=jnp.int32)).reshape(-1).astype(jnp.int32)


def place_ends(array, own_key, least, largest):
    spot = [jax.random.randint(jax.random.fold_in(own_key, axis), (), 0, length) for axis, length in enumerate(array.shape)]
    main_axis = array.shape.index(max(array.shape))
    beside = spot[:main_axis] + [(spot[main_axis] + 1) % array.shape[main_axis]] + spot[main_axis + 1:]
    return array.at[tuple(spot)].set(least).at[tuple(beside)].set(largest)


def levels(key, dims, split, smallest, largest):
    loudness, own = 1.0, jax.random.fold_in(key, 6)
    for position, blocks in split:
        draws = jnp.exp(jax.random.uniform(jax.random.fold_in(own, position), (blocks,), jnp.float32, smallest / len(split), largest / len(split)))
        loudness = loudness * jnp.repeat(draws, dims[position] // blocks).reshape([-1 if axis == position else 1 for axis in range(len(dims))])
    return loudness


def scatter_about(own_key, extent, scale, most, cuts=(), kind=jnp.bfloat16):
    array = scale * jax.random.normal(own_key, extent, jnp.float32)
    if cuts:
        array = array * levels(own_key, extent, cuts, -0.22, 0.18)
    return jnp.clip(array, -most, most).astype(kind)


def setup_inputs(seed: int = 0) -> dict:
    seeds = jax.random.split(jax.random.key(seed), 9)
    return {
        "features": scatter_about(seeds[0], (NODES, F_IN), 1.0, 6.0, ((0, 32),)),
        "tile_counts": draw_tile_counts(jax.random.fold_in(seeds[8], 71), 0),
        "tile_row": place_ends(jax.random.randint(seeds[2], (TILES,), 0, NODES_DEV // BLOCK), jax.random.fold_in(seeds[2], 1), 0, (NODES_DEV // BLOCK) - 1).astype(jnp.int32),
        "tile_col": draw_tile_col(jax.random.fold_in(seeds[8], 71), 0),
        "label_ids": draw_label_ids(jax.random.fold_in(seeds[8], 71), 0),
        "cotangent": scatter_about(seeds[5], (NODES, HID), 1.0, 6.0, ((0, 32),)),
        "self_weight": scatter_about(seeds[6], (F_IN, HID), F_IN ** -0.5, 0.5),
        "neigh_weight": scatter_about(seeds[7], (F_IN, HID), F_IN ** -0.5, 0.5),
    }


edge_moment = 14.0 / 96.0


def reference(features, tile_counts, tile_row, tile_col, label_ids, cotangent, self_weight, neigh_weight):
    row_blocks = NODES_DEV // BLOCK
    scale = (edge_moment * TILE_DEV * N_REP * BLOCK / row_blocks) ** -0.5
    group_tiles = TILE_DEV * N_REP
    counts = tile_counts.reshape(N_ROWS, group_tiles, BLOCK, BLOCK)
    rows_of = tile_row.reshape(N_ROWS, group_tiles)
    cols_of = tile_col.reshape(N_ROWS, group_tiles)
    feature_blocks = features.reshape(NODES // BLOCK, BLOCK, F_IN)

    def gather_group(inputs):
        count_part, row_part, col_part = inputs
        panels = feature_blocks[col_part].astype(jnp.float32)
        products = jnp.einsum('tij,tjf->tif', count_part.astype(jnp.float32), panels, precision=lax.Precision.HIGHEST)
        owner_table = (row_part[:, None] == jnp.arange(row_blocks, dtype=jnp.int32)[None, :]).astype(jnp.float32)
        return jnp.einsum('tr,tif->rif', owner_table, products, precision=lax.Precision.HIGHEST)

    summed = lax.map(gather_group, (counts, rows_of, cols_of)).reshape(NODES, F_IN)
    neighbour = (scale * summed).astype(jnp.bfloat16)
    preact = jnp.dot(features, self_weight, preferred_element_type=jnp.float32) + jnp.dot(neighbour, neigh_weight, preferred_element_type=jnp.float32)
    activation = jax.nn.silu(preact).astype(jnp.bfloat16)
    label_mask = jnp.zeros((NODES,), jnp.float32).at[label_ids].set(1.0)
    masked = cotangent.astype(jnp.float32) * label_mask[:, None]
    sigma = jax.nn.sigmoid(preact)
    delta = (masked * sigma * (1.0 + preact * (1.0 - sigma))).astype(jnp.bfloat16)
    grad_scale = float(LABELS) ** -0.5
    grad_self = grad_scale * jnp.einsum('nf,nh->fh', features.astype(jnp.float32), delta.astype(jnp.float32), precision=lax.Precision.HIGHEST)
    grad_neigh = grad_scale * jnp.einsum('nf,nh->fh', neighbour.astype(jnp.float32), delta.astype(jnp.float32), precision=lax.Precision.HIGHEST)
    back = jnp.einsum('nh,fh->nf', delta.astype(jnp.float32), neigh_weight.astype(jnp.float32), precision=lax.Precision.HIGHEST).astype(jnp.bfloat16)
    back_blocks = back.reshape(N_ROWS, row_blocks, BLOCK, F_IN)

    def spread(total, inputs):
        count_part, row_part, col_part, back_part = inputs
        picked = back_part[row_part].astype(jnp.float32)
        terms = jnp.einsum('tij,tif->tjf', count_part.astype(jnp.float32), picked, precision=lax.Precision.HIGHEST)
        rounded = lax.optimization_barrier(terms.astype(jnp.bfloat16))
        return total.at[col_part].add(rounded.astype(jnp.float32)), None

    start_total = jnp.zeros((NODES // BLOCK, BLOCK, F_IN), jnp.float32)
    total, unused = lax.scan(spread, start_total, (counts, rows_of, cols_of, back_blocks))
    own_term = jnp.einsum('nh,fh->nf', delta.astype(jnp.float32), self_weight.astype(jnp.float32), precision=lax.Precision.HIGHEST)
    grad_features = own_term + scale * total.reshape(NODES, F_IN)
    return (activation, grad_features, grad_self, grad_neigh)
```

```python
import functools

import jax
import jax.numpy as jnp
from jax import lax
from jax.experimental import pallas as pl
from jax.experimental.pallas import tpu as pltpu
from jax.sharding import PartitionSpec as P

edge_moment = 14.0 / 96.0
MESH = pl.DeviceIdType.MESH
NT = (((1,), (1,)), ((), ()))
TN = (((0,), (0,)), ((), ()))


def dot(a, b, dims=(((1,), (0,)), ((), ()))):
    return lax.dot_general(a, b, dims, preferred_element_type=jnp.float32)


def build_kernel(row_s, col_s, counts_ref, a_ref, acc, *, per_step, rep_count, per_half, block):
    step = pl.program_id(0)

    @pl.when(step == 0)
    def _():
        acc[...] = jnp.zeros_like(acc)

    for u in range(per_step):
        t = step * per_step + u
        col = col_s[t]
        place = col // (rep_count * per_half) * per_half + col % per_half
        rows = pl.ds(pl.multiple_of(row_s[t] * block, block), block)
        acc[place, rows, :] += counts_ref[u]

    @pl.when(step == pl.num_programs(0) - 1)
    def _():
        def put(j, carry):
            cols = pl.ds(pl.multiple_of(j * block, block), block)
            a_ref[:, cols] = acc[j].astype(jnp.float32).astype(jnp.bfloat16)
            return carry

        lax.fori_loop(0, acc.shape[0], put, 0, unroll=4)


def build_adjacency(tile_counts, tile_row, tile_col, row_blocks, col_blocks, rep_count, per_half):
    tiles, block, _ = tile_counts.shape
    per_step = 16 if tiles % 16 == 0 else 1
    return pl.pallas_call(
        functools.partial(
            build_kernel, per_step=per_step, rep_count=rep_count, per_half=per_half, block=block
        ),
        out_shape=jax.ShapeDtypeStruct((row_blocks * block, col_blocks * block), jnp.bfloat16),
        grid_spec=pltpu.PrefetchScalarGridSpec(
            num_scalar_prefetch=2,
            grid=(tiles // per_step,),
            in_specs=[pl.BlockSpec((per_step, block, block), lambda s, r, c: (s, 0, 0))],
            out_specs=pl.BlockSpec(
                (row_blocks * block, col_blocks * block), lambda s, r, c: (0, 0)
            ),
            scratch_shapes=[pltpu.VMEM((col_blocks, row_blocks * block, block), jnp.int32)],
        ),
        compiler_params=pltpu.CompilerParams(dimension_semantics=("arbitrary",)),
        name="build_adjacency",
    )(tile_row, tile_col, tile_counts)


def layer_kernel(
    n, zs, ps, scale, grad_scale,
    feat, adj, ids, cot, ws, wn,
    act_out, grad_out, self_out, neigh_out,
    gath, part, part_in, bt, tt, r1, s2, r2, wpart, win, wc, wr1, wz, wo,
    ag_s, ag_r, pair_s, pair_r, r1_s, r1_r, r2_s, r2_r, w1_s, w1_r, wz_s, wz_r, wo_s, wo_r,
):
    me = lax.axis_index("rows")
    rep = lax.axis_index("rep")
    other = 1 - rep
    mz, mp = me // ps, me % ps
    half, f_in = feat.shape

    def zrow(d):
        return (mz + d) % zs

    def prow(d):
        return (mp + d) % ps

    def send(src, dst, ssem, rsem, row, core):
        copy = pltpu.make_async_remote_copy(
            src_ref=src, dst_ref=dst, send_sem=ssem, recv_sem=rsem,
            device_id=(row, core), device_id_type=MESH,
        )
        copy.start()
        sent.append(copy)
        return copy

    def arrived(dst, ssem, rsem):
        pltpu.make_async_remote_copy(
            src_ref=dst, dst_ref=dst, send_sem=ssem, recv_sem=rsem,
            device_id=(me, other), device_id_type=MESH,
        ).wait_recv()

    sent = []
    barrier = pltpu.get_barrier_semaphore()
    for d in range(1, zs):
        pl.semaphore_signal(barrier, inc=1, device_id=(zrow(d) * ps + mp, rep), device_id_type=MESH)
    for d in range(1, ps):
        pl.semaphore_signal(barrier, inc=1, device_id=(mz * ps + prow(d), rep), device_id_type=MESH)
    pl.semaphore_signal(barrier, inc=1, device_id=(me, other), device_id_type=MESH)
    pl.semaphore_wait(barrier, zs + ps - 1)

    for d in range(1, zs):
        send(feat, gath.at[me], ag_s.at[d - 1], ag_r.at[me], zrow(d) * ps + mp, rep)
    for d in range(1, ps):
        send(feat, gath.at[me], ag_s.at[zs - 2 + d], ag_r.at[me], mz * ps + prow(d), rep)
    gath[me] = feat[...]
    first = dot(feat[...], ws[...])
    near = lax.broadcasted_iota(jnp.int32, (half, ids.shape[1]), 0)
    hits = (near == ids[...] - (me * 2 + rep) * half).astype(jnp.float32)
    masked = cot[...].astype(jnp.float32) * jnp.max(hits, axis=1, keepdims=True)
    for e in range(1, zs):
        src = zrow(zs - e) * ps + mp
        arrived(gath.at[src], ag_s.at[0], ag_r.at[src])
        for d in range(1, ps):
            send(
                gath.at[src], gath.at[src], ag_s.at[zs - 2 + e * (ps - 1) + d], ag_r.at[src],
                mz * ps + prow(d), rep,
            )
    for e in range(zs):
        for d in range(1, ps):
            src = zrow(zs - e) * ps + prow(ps - d)
            arrived(gath.at[src], ag_s.at[0], ag_r.at[src])

    chunk = min(n, 16)
    cols = chunk * half

    def forward(c, total):
        left = adj[:, pl.ds(pl.multiple_of(c * cols, cols), cols)]
        right = gath[pl.ds(c * chunk, chunk)].reshape(cols, f_in)
        return total + dot(left, right)

    if n == chunk:
        total = dot(adj[...], gath[...].reshape(cols, f_in))
    else:
        total = lax.fori_loop(0, n // chunk, forward, jnp.zeros((2 * half, f_in), jnp.float32))
    part[...] = total.reshape(2, half, f_in)
    send(part.at[other], part_in, pair_s.at[0], pair_r.at[0], me, other)
    arrived(part_in, pair_s.at[0], pair_r.at[0])
    neighbour = (scale * (part[rep] + part_in[...])).astype(jnp.bfloat16)
    preact = first + dot(neighbour, wn[...])
    sigma = jax.nn.sigmoid(preact)
    act_out[...] = (preact * sigma).astype(jnp.bfloat16)
    delta = (masked * sigma * (1.0 + preact * (1.0 - sigma))).astype(jnp.bfloat16)
    bt[rep] = dot(wn[...], delta, NT).astype(jnp.bfloat16)
    send(bt.at[rep], bt.at[rep], pair_s.at[1], pair_r.at[1], me, other)
    wpart[0] = dot(feat[...], delta, TN)
    wpart[1] = dot(neighbour, delta, TN)
    send(wpart.at[other], win, pair_s.at[2], pair_r.at[2], me, other)
    own_term = dot(delta, ws[...], NT)

    arrived(bt.at[other], pair_s.at[1], pair_r.at[1])
    back = jnp.concatenate([bt[0], bt[1]], axis=1)

    def backward(c):
        out = dot(back, adj[:, pl.ds(pl.multiple_of(c * cols, cols), cols)])
        for j in range(chunk):
            tt[c * chunk + j] = out[:, j * half : (j + 1) * half].astype(jnp.bfloat16)

    if n == chunk:
        out = dot(back, adj[...])
        for j in range(n):
            tt[j] = out[:, j * half : (j + 1) * half].astype(jnp.bfloat16)
    else:
        pl.loop(0, n // chunk)(backward)

    arrived(win, pair_s.at[2], pair_r.at[2])
    wc[...] = (wpart[rep] + win[...]).reshape(wc.shape)
    for d in range(1, ps):
        send(
            wc.at[prow(d)], wr1.at[d - 1], w1_s.at[d - 1], w1_r.at[d - 1], mz * ps + prow(d), rep
        )
    for e in range(1, zs + 1):
        zt = zrow(e)
        for d in range(1, ps):
            k = zt * (ps - 1) + d - 1
            send(
                tt.at[zt * ps + prow(d)], r1.at[k], r1_s.at[(e - 1) * (ps - 1) + d - 1],
                r1_r.at[k], mz * ps + prow(d), rep,
            )
    shard = wc[mp]
    for d in range(1, ps):
        arrived(wr1.at[d - 1], w1_s.at[0], w1_r.at[d - 1])
        shard = shard + wr1[d - 1]
    wz[mz] = shard
    for d in range(1, zs):
        send(wz.at[mz], wz.at[mz], wz_s.at[d - 1], wz_r.at[mz], zrow(d) * ps + mp, rep)

    def plane_sum(zt):
        total = tt[zt * ps + mp].astype(jnp.float32)
        for d in range(1, ps):
            k = zt * (ps - 1) + d - 1
            arrived(r1.at[k], r1_s.at[0], r1_r.at[k])
            total = total + r1[k].astype(jnp.float32)
        return total

    for e in range(1, zs):
        s2[e - 1] = plane_sum(zrow(e)).astype(jnp.bfloat16)
        send(s2.at[e - 1], r2.at[e - 1], r2_s.at[e - 1], r2_r.at[e - 1], zrow(e) * ps + mp, rep)
    for d in range(1, zs):
        src = zrow(d)
        arrived(wz.at[src], wz_s.at[0], wz_r.at[src])
    shard = wz[0]
    for k in range(1, zs):
        shard = shard + wz[k]
    wo[rep, mp] = grad_scale * shard
    for d in range(1, ps):
        send(
            wo.at[rep, mp], wo.at[rep, mp], wo_s.at[d - 1], wo_r.at[mp], mz * ps + prow(d), rep
        )
    total = plane_sum(mz)
    for e in range(1, zs):
        arrived(r2.at[e - 1], r2_s.at[0], r2_r.at[e - 1])
        total = total + r2[e - 1].astype(jnp.float32)
    for d in range(1, ps):
        src = prow(d)
        arrived(wo.at[rep, src], wo_s.at[0], wo_r.at[src])
    send(wo.at[rep], wo.at[rep], pair_s.at[3], pair_r.at[3], me, other)
    grad_out[...] = own_term + scale * jnp.transpose(total)
    arrived(wo.at[other], pair_s.at[3], pair_r.at[3])
    self_out[...] = wo[0].reshape(self_out.shape)
    neigh_out[...] = wo[1].reshape(neigh_out.shape)
    for copy in sent:
        copy.wait_send()


def plane_size(n, width):
    return max(d for d in range(1, n + 1) if n % d == 0 and d * d <= 2 * n and width % (8 * d) == 0)


def shards(
    features, tile_counts, tile_row, tile_col, label_ids, cotangent, self_weight, neigh_weight
):
    half, f_in = features.shape
    hid = cotangent.shape[1]
    tile_total, block, _ = tile_counts.shape
    rep_count = lax.axis_size("rep")
    n = lax.axis_size("rows")
    per_half = half // block
    row_blocks = rep_count * per_half
    scale = (edge_moment * tile_total * rep_count * block / row_blocks) ** (-0.5)
    grad_scale = float(label_ids.shape[0] * n * rep_count) ** (-0.5)
    adj = build_adjacency(
        tile_counts, tile_row, tile_col, row_blocks, n * per_half, rep_count, per_half
    )
    ps = plane_size(n, f_in)
    zs = n // ps
    bf, f4 = jnp.bfloat16, jnp.float32
    dma = pltpu.SemaphoreType.DMA
    vmem = pl.BlockSpec(memory_space=pltpu.VMEM)
    return pl.pallas_call(
        functools.partial(layer_kernel, n, zs, ps, scale, grad_scale),
        out_shape=(
            jax.ShapeDtypeStruct((half, hid), bf),
            jax.ShapeDtypeStruct((half, f_in), f4),
            jax.ShapeDtypeStruct((f_in, hid), f4),
            jax.ShapeDtypeStruct((f_in, hid), f4),
        ),
        in_specs=[vmem] * 6,
        out_specs=(vmem,) * 4,
        scratch_shapes=[
            pltpu.VMEM((n, half, f_in), bf),
            pltpu.VMEM((2, half, f_in), f4),
            pltpu.VMEM((half, f_in), f4),
            pltpu.VMEM((2, f_in, half), bf),
            pltpu.VMEM((n, f_in, half), bf),
            pltpu.VMEM((zs * (ps - 1), f_in, half), bf),
            pltpu.VMEM((zs - 1, f_in, half), bf),
            pltpu.VMEM((zs - 1, f_in, half), bf),
            pltpu.VMEM((2, f_in, hid), f4),
            pltpu.VMEM((f_in, hid), f4),
            pltpu.VMEM((ps, f_in // ps, hid), f4),
            pltpu.VMEM((ps - 1, f_in // ps, hid), f4),
            pltpu.VMEM((zs, f_in // ps, hid), f4),
            pltpu.VMEM((2, ps, f_in // ps, hid), f4),
            dma((n,)), dma((n,)), dma((4,)), dma((4,)),
            dma((zs * (ps - 1),)), dma((zs * (ps - 1),)), dma((zs - 1,)), dma((zs - 1,)),
            dma((ps - 1,)), dma((ps - 1,)), dma((zs - 1,)), dma((zs,)),
            dma((ps - 1,)), dma((ps,)),
        ],
        compiler_params=pltpu.CompilerParams(
            collective_id=0, has_side_effects=True, vmem_limit_bytes=48 * 1024 * 1024
        ),
        name="layer",
    )(features, adj, label_ids.reshape(1, -1), cotangent, self_weight, neigh_weight)


def solution(mesh):
    placed = (
        P(("rows", "rep"), None),
        P(("rows", "rep"), None, None),
        P(("rows", "rep")),
        P(("rows", "rep")),
        P(("rows", "rep")),
        P(("rows", "rep"), None),
        P(),
        P(),
    )
    return jax.shard_map(
        shards,
        mesh=mesh,
        in_specs=placed,
        out_specs=(P(("rows", "rep"), None), P(("rows", "rep"), None), P(), P()),
        check_vma=False,
    )
```

```python
import functools

import jax
import jax.numpy as jnp
from jax import lax
from jax.experimental import pallas as pl
from jax.experimental.pallas import tpu as pltpu
from jax.sharding import PartitionSpec as P

edge_moment = 14.0 / 96.0
MESH = pl.DeviceIdType.MESH
NT = (((1,), (1,)), ((), ()))
TN = (((0,), (0,)), ((), ()))


def dot(a, b, dims=(((1,), (0,)), ((), ()))):
    return lax.dot_general(a, b, dims, preferred_element_type=jnp.float32)


def build_kernel(row_s, col_s, counts, a_ref, buf, acc, sems, *, rep_count, per_half, block):
    parts = sems.shape[0]
    size = buf.shape[0] // parts

    def fetch(c):
        span = pl.ds(c * size, size)
        return pltpu.make_async_copy(counts.at[span], buf.at[span], sems.at[c])

    for c in range(parts):
        fetch(c).start()
    acc[...] = jnp.zeros_like(acc)
    group = 8 if size % 8 == 0 else 1
    for c in range(parts):
        fetch(c).wait()

        @pl.loop(0, size // group)
        def _(g):
            for u in range(group):
                t = c * size + g * group + u
                col = col_s[t]
                place = col // (rep_count * per_half) * per_half + col % per_half
                rows = pl.ds(pl.multiple_of(row_s[t] * block, block), block)
                acc[place, rows, :] += buf[t]

    def put(j, carry):
        cols = pl.ds(pl.multiple_of(j * block, block), block)
        a_ref[:, cols] = acc[j].astype(jnp.float32).astype(jnp.bfloat16)
        return carry

    lax.fori_loop(0, acc.shape[0], put, 0, unroll=4)


def build_adjacency(tile_counts, tile_row, tile_col, row_blocks, col_blocks, rep_count, per_half):
    tiles, block, _ = tile_counts.shape
    parts = 16 if tiles % 16 == 0 else 1
    return pl.pallas_call(
        functools.partial(build_kernel, rep_count=rep_count, per_half=per_half, block=block),
        out_shape=jax.ShapeDtypeStruct((row_blocks * block, col_blocks * block), jnp.bfloat16),
        grid_spec=pltpu.PrefetchScalarGridSpec(
            num_scalar_prefetch=2,
            grid=(),
            in_specs=[pl.BlockSpec(memory_space=pl.ANY)],
            out_specs=pl.BlockSpec(memory_space=pltpu.VMEM),
            scratch_shapes=[
                pltpu.VMEM((tiles, block, block), jnp.int32),
                pltpu.VMEM((col_blocks, row_blocks * block, block), jnp.int32),
                pltpu.SemaphoreType.DMA((parts,)),
            ],
        ),
        compiler_params=pltpu.CompilerParams(vmem_limit_bytes=59 * 1024 * 1024),
        name="build_adjacency",
    )(tile_row, tile_col, tile_counts)


def finish_kernel(*refs):
    count = len(refs) // 2
    sems = refs[-1]
    copies = [
        pltpu.make_async_copy(refs[k], refs[count + k], sems.at[k]) for k in range(count)
    ]
    for copy in copies:
        copy.start()
    for copy in copies:
        copy.wait()


def finish(arrays):
    return pl.pallas_call(
        finish_kernel,
        out_shape=tuple(jax.ShapeDtypeStruct(a.shape, a.dtype) for a in arrays),
        in_specs=[pl.BlockSpec(memory_space=pltpu.VMEM)] * len(arrays),
        out_specs=tuple(pl.BlockSpec(memory_space=pl.ANY) for _ in arrays),
        scratch_shapes=[pltpu.SemaphoreType.DMA((len(arrays),))],
        compiler_params=pltpu.CompilerParams(vmem_limit_bytes=4 * 1024 * 1024),
        name="finish",
    )(*arrays)


def layer_kernel(
    n, zs, ps, scale, grad_scale,
    feat, adj, ids, cot, ws, wn,
    act_out, grad_out, self_out, neigh_out,
    gath, part, part_in, bt, tt, r1, s2, r2, wpart, win, wc, wr1, wz, wo,
    ag_s, ag_r, pair_s, pair_r, r1_s, r1_r, r2_s, r2_r, w1_s, w1_r, wz_s, wz_r, wo_s, wo_r,
):
    me = lax.axis_index("rows")
    rep = lax.axis_index("rep")
    other = 1 - rep
    mz, mp = me // ps, me % ps
    half, f_in = feat.shape

    def zrow(d):
        return (mz + d) % zs

    def prow(d):
        return (mp + d) % ps

    def send(src, dst, ssem, rsem, row, core):
        copy = pltpu.make_async_remote_copy(
            src_ref=src, dst_ref=dst, send_sem=ssem, recv_sem=rsem,
            device_id=(row, core), device_id_type=MESH,
        )
        copy.start()
        sent.append(copy)
        return copy

    def arrived(dst, ssem, rsem):
        pltpu.make_async_remote_copy(
            src_ref=dst, dst_ref=dst, send_sem=ssem, recv_sem=rsem,
            device_id=(me, other), device_id_type=MESH,
        ).wait_recv()

    sent = []
    barrier = pltpu.get_barrier_semaphore()
    for d in range(1, zs):
        pl.semaphore_signal(barrier, inc=1, device_id=(zrow(d) * ps + mp, rep), device_id_type=MESH)
    for d in range(1, ps):
        for core in (rep, other):
            pl.semaphore_signal(
                barrier, inc=1, device_id=(mz * ps + prow(d), core), device_id_type=MESH
            )
    pl.semaphore_signal(barrier, inc=1, device_id=(me, other), device_id_type=MESH)
    pl.semaphore_wait(barrier, zs + 2 * (ps - 1))

    for d in range(1, zs):
        send(feat, gath.at[me], ag_s.at[d - 1], ag_r.at[me], zrow(d) * ps + mp, rep)
    for d in range(1, ps):
        send(feat, gath.at[me], ag_s.at[zs - 2 + d], ag_r.at[me], mz * ps + prow(d), rep)
    gath[me] = feat[...]
    first = dot(feat[...], ws[...])
    near = lax.broadcasted_iota(jnp.int32, (half, ids.shape[1]), 0)
    hits = (near == ids[...] - (me * 2 + rep) * half).astype(jnp.float32)
    masked = cot[...].astype(jnp.float32) * jnp.max(hits, axis=1, keepdims=True)
    for e in range(1, zs):
        src = zrow(zs - e) * ps + mp
        arrived(gath.at[src], ag_s.at[0], ag_r.at[src])
        for d in range(1, ps):
            send(
                gath.at[src], gath.at[src], ag_s.at[zs - 2 + e * (ps - 1) + d], ag_r.at[src],
                mz * ps + prow(d), rep,
            )
    span = ps * half

    def plane_cols(zt):
        return adj[:, pl.ds(pl.multiple_of(zt * span, span), span)]

    total = jnp.zeros((2 * half, f_in), jnp.float32)
    for e in range(zs):
        zt = zrow(zs - e)
        for d in range(1, ps):
            src = zt * ps + prow(ps - d)
            arrived(gath.at[src], ag_s.at[0], ag_r.at[src])
        total = total + dot(plane_cols(zt), gath[pl.ds(zt * ps, ps)].reshape(span, f_in))
    part[...] = total.reshape(2, half, f_in)
    send(part.at[other], part_in, pair_s.at[0], pair_r.at[0], me, other)
    arrived(part_in, pair_s.at[0], pair_r.at[0])
    neighbour = (scale * (part[rep] + part_in[...])).astype(jnp.bfloat16)
    preact = first + dot(neighbour, wn[...])
    sigma = jax.nn.sigmoid(preact)
    act_out[...] = (preact * sigma).astype(jnp.bfloat16)
    delta = (masked * sigma * (1.0 + preact * (1.0 - sigma))).astype(jnp.bfloat16)
    bt[rep] = dot(wn[...], delta, NT).astype(jnp.bfloat16)
    send(bt.at[rep], bt.at[rep], pair_s.at[1], pair_r.at[1], me, other)
    wpart[0] = dot(feat[...], delta, TN)
    wpart[1] = dot(neighbour, delta, TN)
    send(wpart.at[other], win, pair_s.at[2], pair_r.at[2], me, other)
    own_term = dot(delta, ws[...], NT)

    arrived(bt.at[other], pair_s.at[1], pair_r.at[1])
    back = jnp.concatenate([bt[0], bt[1]], axis=1)

    def products(e):
        zt = zrow(e)
        out = dot(back, plane_cols(zt))
        for j in range(ps):
            tt[zt * ps + j] = out[:, j * half : (j + 1) * half].astype(jnp.bfloat16)
        for d in range(1, ps):
            k = zt * (ps - 1) + d - 1
            send(
                tt.at[zt * ps + prow(d)], r1.at[k], r1_s.at[(e - 1) * (ps - 1) + d - 1],
                r1_r.at[k], mz * ps + prow(d), rep,
            )

    products(1)
    arrived(win, pair_s.at[2], pair_r.at[2])
    wc[...] = (wpart[rep] + win[...]).astype(jnp.bfloat16).reshape(wc.shape)
    for d in range(1, ps):
        send(
            wc.at[prow(d)], wr1.at[d - 1], w1_s.at[d - 1], w1_r.at[d - 1], mz * ps + prow(d), rep
        )
    for e in range(2, zs + 1):
        products(e)
    shard = wc[mp].astype(jnp.float32)
    for d in range(1, ps):
        arrived(wr1.at[d - 1], w1_s.at[0], w1_r.at[d - 1])
        shard = shard + wr1[d - 1].astype(jnp.float32)
    wz[mz] = shard.astype(jnp.bfloat16)
    for d in range(1, zs):
        send(wz.at[mz], wz.at[mz], wz_s.at[d - 1], wz_r.at[mz], zrow(d) * ps + mp, rep)

    def plane_sum(zt):
        total = tt[zt * ps + mp].astype(jnp.float32)
        for d in range(1, ps):
            k = zt * (ps - 1) + d - 1
            arrived(r1.at[k], r1_s.at[0], r1_r.at[k])
            total = total + r1[k].astype(jnp.float32)
        return total

    for e in range(1, zs):
        s2[e - 1] = plane_sum(zrow(e)).astype(jnp.bfloat16)
        send(s2.at[e - 1], r2.at[e - 1], r2_s.at[e - 1], r2_r.at[e - 1], zrow(e) * ps + mp, rep)
    for d in range(1, zs):
        src = zrow(d)
        arrived(wz.at[src], wz_s.at[0], wz_r.at[src])
    shard = wz[0].astype(jnp.float32)
    for k in range(1, zs):
        shard = shard + wz[k].astype(jnp.float32)
    wo[rep, mp] = (grad_scale * shard).astype(jnp.bfloat16)
    send(wo.at[rep, mp], wo.at[rep, mp], wo_s.at[0], wo_r.at[rep, mp], me, other)
    for d in range(1, ps):
        for c, core in enumerate((rep, other)):
            send(
                wo.at[rep, mp], wo.at[rep, mp], wo_s.at[2 * d - 1 + c], wo_r.at[rep, mp],
                mz * ps + prow(d), core,
            )
    total = plane_sum(mz)
    for e in range(1, zs):
        arrived(r2.at[e - 1], r2_s.at[0], r2_r.at[e - 1])
        total = total + r2[e - 1].astype(jnp.float32)
    grad_out[...] = own_term + scale * jnp.transpose(total)
    arrived(wo.at[other, mp], wo_s.at[0], wo_r.at[other, mp])
    for d in range(1, ps):
        src = prow(d)
        for core in (rep, other):
            arrived(wo.at[core, src], wo_s.at[0], wo_r.at[core, src])
    self_out[...] = wo[0].astype(jnp.float32).reshape(self_out.shape)
    neigh_out[...] = wo[1].astype(jnp.float32).reshape(neigh_out.shape)
    for copy in sent:
        copy.wait_send()


def plane_size(n, width):
    return max(d for d in range(1, n + 1) if n % d == 0 and d * d <= 2 * n and width % (8 * d) == 0)


def shards(
    features, tile_counts, tile_row, tile_col, label_ids, cotangent, self_weight, neigh_weight
):
    half, f_in = features.shape
    hid = cotangent.shape[1]
    tile_total, block, _ = tile_counts.shape
    rep_count = lax.axis_size("rep")
    n = lax.axis_size("rows")
    per_half = half // block
    row_blocks = rep_count * per_half
    scale = (edge_moment * tile_total * rep_count * block / row_blocks) ** (-0.5)
    grad_scale = float(label_ids.shape[0] * n * rep_count) ** (-0.5)
    adj = build_adjacency(
        tile_counts, tile_row, tile_col, row_blocks, n * per_half, rep_count, per_half
    )
    ps = plane_size(n, f_in)
    zs = n // ps
    bf, f4 = jnp.bfloat16, jnp.float32
    dma = pltpu.SemaphoreType.DMA
    vmem = pl.BlockSpec(memory_space=pltpu.VMEM)
    outs = pl.pallas_call(
        functools.partial(layer_kernel, n, zs, ps, scale, grad_scale),
        out_shape=(
            jax.ShapeDtypeStruct((half, hid), bf),
            jax.ShapeDtypeStruct((half, f_in), f4),
            jax.ShapeDtypeStruct((f_in, hid), f4),
            jax.ShapeDtypeStruct((f_in, hid), f4),
        ),
        in_specs=[vmem] * 6,
        out_specs=(vmem,) * 4,
        scratch_shapes=[
            pltpu.VMEM((n, half, f_in), bf),
            pltpu.VMEM((2, half, f_in), f4),
            pltpu.VMEM((half, f_in), f4),
            pltpu.VMEM((2, f_in, half), bf),
            pltpu.VMEM((n, f_in, half), bf),
            pltpu.VMEM((zs * (ps - 1), f_in, half), bf),
            pltpu.VMEM((zs - 1, f_in, half), bf),
            pltpu.VMEM((zs - 1, f_in, half), bf),
            pltpu.VMEM((2, f_in, hid), f4),
            pltpu.VMEM((f_in, hid), f4),
            pltpu.VMEM((ps, f_in // ps, hid), bf),
            pltpu.VMEM((ps - 1, f_in // ps, hid), bf),
            pltpu.VMEM((zs, f_in // ps, hid), bf),
            pltpu.VMEM((2, ps, f_in // ps, hid), bf),
            dma((n,)), dma((n,)), dma((3,)), dma((3,)),
            dma((zs * (ps - 1),)), dma((zs * (ps - 1),)), dma((zs - 1,)), dma((zs - 1,)),
            dma((ps - 1,)), dma((ps - 1,)), dma((zs - 1,)), dma((zs,)),
            dma((2 * ps - 1,)), dma((2, ps)),
        ],
        compiler_params=pltpu.CompilerParams(
            collective_id=0, has_side_effects=True, vmem_limit_bytes=48 * 1024 * 1024
        ),
        name="layer",
    )(features, adj, label_ids.reshape(1, -1), cotangent, self_weight, neigh_weight)
    return finish(outs)


def solution(mesh):
    placed = (
        P(("rows", "rep"), None),
        P(("rows", "rep"), None, None),
        P(("rows", "rep")),
        P(("rows", "rep")),
        P(("rows", "rep")),
        P(("rows", "rep"), None),
        P(),
        P(),
    )
    return jax.shard_map(
        shards,
        mesh=mesh,
        in_specs=placed,
        out_specs=(P(("rows", "rep"), None), P(("rows", "rep"), None), P(), P()),
        check_vma=False,
    )
```

```python
import functools

import jax
import jax.numpy as jnp
from jax import lax
from jax.experimental import pallas as pl
from jax.experimental.pallas import tpu as pltpu
from jax.sharding import PartitionSpec as P

edge_moment = 14.0 / 96.0
MESH = pl.DeviceIdType.MESH
NT = (((1,), (1,)), ((), ()))
TN = (((0,), (0,)), ((), ()))


def dot(a, b, dims=(((1,), (0,)), ((), ()))):
    return lax.dot_general(a, b, dims, preferred_element_type=jnp.float32)


def table_kernel(row_s, col_s, table, filled, *, rep_count, cap):
    tiles = row_s.shape[0]
    group = 8 if tiles % 8 == 0 else 1

    @pl.loop(0, filled.shape[0])
    def _(j):
        filled[j] = 0
        for k in range(cap):
            table[j * cap + k] = 2 * tiles

    @pl.loop(0, tiles // group)
    def _(g):
        for u in range(group):
            t = g * group + u
            owner = col_s[t] // rep_count
            have = filled[owner]
            table[owner * cap + have] = 2 * t + row_s[t]
            filled[owner] = have + 1


def slot_table(tile_row, tile_col, n, rep_count, cap):
    return pl.pallas_call(
        functools.partial(table_kernel, rep_count=rep_count, cap=cap),
        out_shape=jax.ShapeDtypeStruct((n * cap,), jnp.int32),
        grid_spec=pltpu.PrefetchScalarGridSpec(
            num_scalar_prefetch=2,
            grid=(),
            in_specs=[],
            out_specs=pl.BlockSpec(memory_space=pltpu.SMEM),
            scratch_shapes=[pltpu.SMEM((n,), jnp.int32)],
        ),
        compiler_params=pltpu.CompilerParams(vmem_limit_bytes=60 * 1024 * 1024),
        cost_estimate=pl.CostEstimate(flops=1 << 33, bytes_accessed=1 << 24, transcendentals=0),
        name="slot_table",
    )(tile_row, tile_col)


def finish_kernel(*refs):
    count = len(refs) // 2
    sems = refs[-1]
    copies = [
        pltpu.make_async_copy(refs[k], refs[count + k], sems.at[k]) for k in range(count)
    ]
    for copy in copies:
        copy.start()
    for copy in copies:
        copy.wait()


def finish(arrays):
    return pl.pallas_call(
        finish_kernel,
        out_shape=tuple(jax.ShapeDtypeStruct(a.shape, a.dtype) for a in arrays),
        in_specs=[pl.BlockSpec(memory_space=pltpu.VMEM)] * len(arrays),
        out_specs=tuple(pl.BlockSpec(memory_space=pl.ANY) for _ in arrays),
        scratch_shapes=[pltpu.SemaphoreType.DMA((len(arrays),))],
        compiler_params=pltpu.CompilerParams(vmem_limit_bytes=4 * 1024 * 1024),
        name="finish",
    )(*arrays)


def layer_kernel(
    n, zs, ps, cap, scale, grad_scale,
    table, counts, feat, ids, cot, ws, wn,
    act_out, grad_out, self_out, neigh_out,
    buf, adj, gath, part, part_in, bt, tt, r1, s2, r2, wpart, win, wc, wr1, wz, wo,
    ag_s, ag_r, pair_s, pair_r, r1_s, r1_r, r2_s, r2_r, w1_s, w1_r, wz_s, wz_r, wo_s, wo_r, tile_s,
):
    me = lax.axis_index("rows")
    rep = lax.axis_index("rep")
    other = 1 - rep
    mz, mp = me // ps, me % ps
    half, f_in = feat.shape

    def zrow(d):
        return (mz + d) % zs

    def prow(d):
        return (mp + d) % ps

    def send(src, dst, ssem, rsem, row, core):
        copy = pltpu.make_async_remote_copy(
            src_ref=src, dst_ref=dst, send_sem=ssem, recv_sem=rsem,
            device_id=(row, core), device_id_type=MESH,
        )
        copy.start()
        sent.append(copy)
        return copy

    def arrived(dst, ssem, rsem):
        pltpu.make_async_remote_copy(
            src_ref=dst, dst_ref=dst, send_sem=ssem, recv_sem=rsem,
            device_id=(me, other), device_id_type=MESH,
        ).wait_recv()

    sent = []
    tiles = counts.shape[0]
    parts = tile_s.shape[0]
    size = tiles // parts
    fetches = []
    for c in range(parts):
        fetches.append(
            pltpu.make_async_copy(
                counts.at[pl.ds(c * size, size)], buf.at[pl.ds(c * size, size)], tile_s.at[c]
            )
        )
        fetches[-1].start()
    barrier = pltpu.get_barrier_semaphore()
    for d in range(1, zs):
        pl.semaphore_signal(barrier, inc=1, device_id=(zrow(d) * ps + mp, rep), device_id_type=MESH)
    for d in range(1, ps):
        for core in (rep, other):
            pl.semaphore_signal(
                barrier, inc=1, device_id=(mz * ps + prow(d), core), device_id_type=MESH
            )
    pl.semaphore_signal(barrier, inc=1, device_id=(me, other), device_id_type=MESH)
    pl.semaphore_wait(barrier, zs + 2 * (ps - 1))

    for d in range(1, zs):
        send(feat, gath.at[me], ag_s.at[d - 1], ag_r.at[me], zrow(d) * ps + mp, rep)
    for d in range(1, ps):
        send(feat, gath.at[me], ag_s.at[zs - 2 + d], ag_r.at[me], mz * ps + prow(d), rep)
    gath[me] = feat[...]
    first = dot(feat[...], ws[...])
    near = lax.broadcasted_iota(jnp.int32, (half, ids.shape[1]), 0)
    hits = (near == ids[...] - (me * 2 + rep) * half).astype(jnp.float32)
    masked = cot[...].astype(jnp.float32) * jnp.max(hits, axis=1, keepdims=True)
    buf[tiles] = jnp.zeros((half, half), jnp.int32)

    def pass_on(e):
        src = zrow(zs - e) * ps + mp
        arrived(gath.at[src], ag_s.at[0], ag_r.at[src])
        for d in range(1, ps):
            send(
                gath.at[src], gath.at[src], ag_s.at[zs - 2 + e * (ps - 1) + d], ag_r.at[src],
                mz * ps + prow(d), rep,
            )

    def build_plane(zt):
        @pl.loop(0, ps)
        def _(q):
            j = zt * ps + q
            both = jnp.zeros((half, half), jnp.int32)
            low = both
            for k in range(cap):
                entry = table[j * cap + k]
                tile = buf[entry // 2]
                both = both + tile
                low = low + tile * (entry % 2)
            cols = pl.ds(pl.multiple_of(j * half, half), half)
            adj[:half, cols] = (both - low).astype(jnp.float32).astype(jnp.bfloat16)
            adj[half:, cols] = low.astype(jnp.float32).astype(jnp.bfloat16)

    pass_on(1)
    for fetch in fetches:
        fetch.wait()
    for e in range(zs):
        build_plane(zrow(zs - e))
        if 2 <= e + 2 < zs:
            pass_on(e + 2)

    span = ps * half

    def plane_cols(zt):
        return adj[:, pl.ds(pl.multiple_of(zt * span, span), span)]

    total = jnp.zeros((2 * half, f_in), jnp.float32)
    for e in range(zs):
        zt = zrow(zs - e)
        for d in range(1, ps):
            src = zt * ps + prow(ps - d)
            arrived(gath.at[src], ag_s.at[0], ag_r.at[src])
        total = total + dot(plane_cols(zt), gath[pl.ds(zt * ps, ps)].reshape(span, f_in))
    part[...] = total.reshape(2, half, f_in)
    send(part.at[other], part_in, pair_s.at[0], pair_r.at[0], me, other)
    arrived(part_in, pair_s.at[0], pair_r.at[0])
    neighbour = (scale * (part[rep] + part_in[...])).astype(jnp.bfloat16)
    preact = first + dot(neighbour, wn[...])
    sigma = jax.nn.sigmoid(preact)
    act_out[...] = (preact * sigma).astype(jnp.bfloat16)
    delta = (masked * sigma * (1.0 + preact * (1.0 - sigma))).astype(jnp.bfloat16)
    bt[rep] = dot(wn[...], delta, NT).astype(jnp.bfloat16)
    send(bt.at[rep], bt.at[rep], pair_s.at[1], pair_r.at[1], me, other)
    wpart[0] = dot(feat[...], delta, TN)
    wpart[1] = dot(neighbour, delta, TN)
    send(wpart.at[other], win, pair_s.at[2], pair_r.at[2], me, other)
    own_term = dot(delta, ws[...], NT)

    arrived(bt.at[other], pair_s.at[1], pair_r.at[1])
    back = jnp.concatenate([bt[0], bt[1]], axis=1)

    def products(e):
        zt = zrow(e)
        out = dot(back, plane_cols(zt))
        for j in range(ps):
            tt[zt * ps + j] = out[:, j * half : (j + 1) * half].astype(jnp.bfloat16)
        for d in range(1, ps):
            k = zt * (ps - 1) + d - 1
            send(
                tt.at[zt * ps + prow(d)], r1.at[k], r1_s.at[(e - 1) * (ps - 1) + d - 1],
                r1_r.at[k], mz * ps + prow(d), rep,
            )

    products(1)
    arrived(win, pair_s.at[2], pair_r.at[2])
    wc[...] = (wpart[rep] + win[...]).astype(jnp.bfloat16).reshape(wc.shape)
    for d in range(1, ps):
        send(
            wc.at[prow(d)], wr1.at[d - 1], w1_s.at[d - 1], w1_r.at[d - 1], mz * ps + prow(d), rep
        )
    for e in range(2, zs + 1):
        products(e)
    shard = wc[mp].astype(jnp.float32)
    for d in range(1, ps):
        arrived(wr1.at[d - 1], w1_s.at[0], w1_r.at[d - 1])
        shard = shard + wr1[d - 1].astype(jnp.float32)
    wz[mz] = shard.astype(jnp.bfloat16)
    for d in range(1, zs):
        send(wz.at[mz], wz.at[mz], wz_s.at[d - 1], wz_r.at[mz], zrow(d) * ps + mp, rep)

    def plane_sum(zt):
        total = tt[zt * ps + mp].astype(jnp.float32)
        for d in range(1, ps):
            k = zt * (ps - 1) + d - 1
            arrived(r1.at[k], r1_s.at[0], r1_r.at[k])
            total = total + r1[k].astype(jnp.float32)
        return total

    for e in range(1, zs):
        s2[e - 1] = plane_sum(zrow(e)).astype(jnp.bfloat16)
        send(s2.at[e - 1], r2.at[e - 1], r2_s.at[e - 1], r2_r.at[e - 1], zrow(e) * ps + mp, rep)
    for d in range(1, zs):
        src = zrow(d)
        arrived(wz.at[src], wz_s.at[0], wz_r.at[src])
    shard = wz[0].astype(jnp.float32)
    for k in range(1, zs):
        shard = shard + wz[k].astype(jnp.float32)
    wo[rep, mp] = (grad_scale * shard).astype(jnp.bfloat16)
    send(wo.at[rep, mp], wo.at[rep, mp], wo_s.at[0], wo_r.at[rep, mp], me, other)
    for d in range(1, ps):
        for c, core in enumerate((rep, other)):
            send(
                wo.at[rep, mp], wo.at[rep, mp], wo_s.at[2 * d - 1 + c], wo_r.at[rep, mp],
                mz * ps + prow(d), core,
            )
    total = plane_sum(mz)
    for e in range(1, zs):
        arrived(r2.at[e - 1], r2_s.at[0], r2_r.at[e - 1])
        total = total + r2[e - 1].astype(jnp.float32)
    grad_out[...] = own_term + scale * jnp.transpose(total)
    arrived(wo.at[other, mp], wo_s.at[0], wo_r.at[other, mp])
    for d in range(1, ps):
        src = prow(d)
        for core in (rep, other):
            arrived(wo.at[core, src], wo_s.at[0], wo_r.at[core, src])
    self_out[...] = wo[0].astype(jnp.float32).reshape(self_out.shape)
    neigh_out[...] = wo[1].astype(jnp.float32).reshape(neigh_out.shape)
    for copy in sent:
        copy.wait_send()


def plane_size(n, width):
    return max(d for d in range(1, n + 1) if n % d == 0 and d * d <= 2 * n and width % (8 * d) == 0)


def shards(
    features, tile_counts, tile_row, tile_col, label_ids, cotangent, self_weight, neigh_weight
):
    half, f_in = features.shape
    hid = cotangent.shape[1]
    tile_total, block, _ = tile_counts.shape
    rep_count = lax.axis_size("rep")
    n = lax.axis_size("rows")
    per_half = half // block
    row_blocks = rep_count * per_half
    scale = (edge_moment * tile_total * rep_count * block / row_blocks) ** (-0.5)
    grad_scale = float(label_ids.shape[0] * n * rep_count) ** (-0.5)
    cap = tile_total * rep_count // n
    parts = 8 if tile_total % 8 == 0 else 1
    table = slot_table(tile_row, tile_col, n, rep_count, cap)
    ps = plane_size(n, f_in)
    zs = n // ps
    bf, f4 = jnp.bfloat16, jnp.float32
    dma = pltpu.SemaphoreType.DMA
    vmem = pl.BlockSpec(memory_space=pltpu.VMEM)
    outs = pl.pallas_call(
        functools.partial(layer_kernel, n, zs, ps, cap, scale, grad_scale),
        out_shape=(
            jax.ShapeDtypeStruct((half, hid), bf),
            jax.ShapeDtypeStruct((half, f_in), f4),
            jax.ShapeDtypeStruct((f_in, hid), f4),
            jax.ShapeDtypeStruct((f_in, hid), f4),
        ),
        in_specs=[pl.BlockSpec(memory_space=pltpu.SMEM), pl.BlockSpec(memory_space=pl.ANY)]
        + [vmem] * 5,
        out_specs=(vmem,) * 4,
        scratch_shapes=[
            pltpu.VMEM((tile_total + 1, block, block), jnp.int32),
            pltpu.VMEM((row_blocks * block, n * block), bf),
            pltpu.VMEM((n, half, f_in), bf),
            pltpu.VMEM((2, half, f_in), f4),
            pltpu.VMEM((half, f_in), f4),
            pltpu.VMEM((2, f_in, half), bf),
            pltpu.VMEM((n, f_in, half), bf),
            pltpu.VMEM((zs * (ps - 1), f_in, half), bf),
            pltpu.VMEM((zs - 1, f_in, half), bf),
            pltpu.VMEM((zs - 1, f_in, half), bf),
            pltpu.VMEM((2, f_in, hid), f4),
            pltpu.VMEM((f_in, hid), f4),
            pltpu.VMEM((ps, f_in // ps, hid), bf),
            pltpu.VMEM((ps - 1, f_in // ps, hid), bf),
            pltpu.VMEM((zs, f_in // ps, hid), bf),
            pltpu.VMEM((2, ps, f_in // ps, hid), bf),
            dma((n,)), dma((n,)), dma((3,)), dma((3,)),
            dma((zs * (ps - 1),)), dma((zs * (ps - 1),)), dma((zs - 1,)), dma((zs - 1,)),
            dma((ps - 1,)), dma((ps - 1,)), dma((zs - 1,)), dma((zs,)),
            dma((2 * ps - 1,)), dma((2, ps)), dma((parts,)),
        ],
        compiler_params=pltpu.CompilerParams(
            collective_id=0, has_side_effects=True, vmem_limit_bytes=50 * 1024 * 1024
        ),
        name="layer",
    )(table, tile_counts, features, label_ids.reshape(1, -1), cotangent, self_weight, neigh_weight)
    return finish(outs)


def solution(mesh):
    placed = (
        P(("rows", "rep"), None),
        P(("rows", "rep"), None, None),
        P(("rows", "rep")),
        P(("rows", "rep")),
        P(("rows", "rep")),
        P(("rows", "rep"), None),
        P(),
        P(),
    )
    return jax.shard_map(
        shards,
        mesh=mesh,
        in_specs=placed,
        out_specs=(P(("rows", "rep"), None), P(("rows", "rep"), None), P(), P()),
        check_vma=False,
    )
```
